32 devices in a mesh: dp: 2 (over core), node: 4 (over z), local: 4 (over y, x).
Axes of the slice: x: 2, y: 2, z: 4, core: 2. Of those that a mesh axis runs over, the one named last changes fastest.
Arguments:
- tokens: bfloat16 [4096, 3584], P(('dp', 'node', 'local')), parts along dimension 0, may hold values from -6 to 6
- gate_scores: float32 [4096, 4], P(('dp', 'node', 'local')), parts along dimension 0, may hold values from 0.1 to 1
- expert_ids: int32 [4096, 4], P(('dp', 'node', 'local')), parts along dimension 0, may hold values from 0 to 15, as said below
- w_gate: bfloat16 [16, 3584, 1024], P(('node', 'local')), may hold values from -0.09375 to 0.09375
- w_up: bfloat16 [16, 3584, 1024], P(('node', 'local')), may hold values from -0.09375 to 0.09375
- w_down: bfloat16 [16, 1024, 3584], P(('node', 'local')), may hold values from -0.1875 to 0.1875
Outputs:
- mixed: bfloat16 [4096, 3584], P(('dp', 'node', 'local')), parts along dimension 0
The draws below stay inside these ranges and needn't reach their ends.
There are 2 independent parts, one for each index of `dp`. The reference program is written for one: setup_inputs(seed, part) draws one part's arguments, and reference() takes and returns one part's arrays. A program takes and returns all parts, laid end to end along the dimension named above; an argument that names none is the same for every part. Nothing has to cross between parts.
Inputs may be any that keep to these rules, and one draw needn't show every extreme that they name: `expert_ids`: expert e belongs to node group e // 4 and lives on the device of index e along node and local together. Each token names 4 different experts in exactly 2 different node groups, at least one in each. The 128 tokens of one device name every node group exactly 64 times, and in every node group one expert is named by all 64 of them, so no expert is named more than 64 times by the tokens of one device.
All inputs are finite; a program needn't handle non-finite values.
Results may differ from the reference program's by a relative error of at most 0.0075.
Values may be sent and summed in bfloat16 or wider, within the bound.
A program may use at most 192 MiB of HBM per device.

```python
import jax
import jax.numpy as jnp
from jax import lax

D = 3584
FF = 1024
TOP = 4
MAXNODES = 2
TOK_DEV = 128
EXPERTS = 16
CAP = 64
TOKENS = 2048
N_NODE = 4
N_LOCAL = 4


def draw_expert_ids(key, part):
    blocks = N_NODE * N_LOCAL
    key_nodes = jax.random.fold_in(key, 11)
    key_order = jax.random.fold_in(key, 12)
    key_hot_one = jax.random.fold_in(key, 13)
    key_hot_two = jax.random.fold_in(key, 14)
    key_pick = jax.random.fold_in(key, 15)
    node_keys = jax.random.randint(key_nodes, (blocks, N_NODE), 0, 1 << 20) * N_NODE + jnp.arange(N_NODE, dtype=jnp.int32)
    node_order = jnp.argsort(node_keys, axis=1).astype(jnp.int32)
    order_keys = jax.random.randint(key_order, (blocks, TOK_DEV), 0, 1 << 20) * TOK_DEV + jnp.arange(TOK_DEV, dtype=jnp.int32)
    token_order = jnp.argsort(order_keys, axis=1).astype(jnp.int32)
    node_slot = (token_order[:, :, None] * MAXNODES + jnp.arange(MAXNODES, dtype=jnp.int32)) % N_NODE
    node_table = jnp.broadcast_to(node_order[:, None, :], (blocks, TOK_DEV, N_NODE))
    chosen_nodes = jnp.take_along_axis(node_table, node_slot, axis=2)
    hot_local = jnp.minimum(jax.random.randint(key_hot_one, (blocks, N_NODE), 0, N_LOCAL), jax.random.randint(key_hot_two, (blocks, N_NODE), 0, N_LOCAL))
    hot_table = jnp.broadcast_to(hot_local[:, None, :], (blocks, TOK_DEV, N_NODE))
    hot_chosen = jnp.take_along_axis(hot_table, chosen_nodes, axis=2)
    local_range = jnp.arange(N_LOCAL, dtype=jnp.int32)
    candidates = (chosen_nodes[..., None] * N_LOCAL + local_range).reshape(blocks, TOK_DEV, MAXNODES * N_LOCAL)
    is_hot = (local_range == hot_chosen[..., None]).astype(jnp.int32).reshape(blocks, TOK_DEV, MAXNODES * N_LOCAL)
    scores = jax.random.randint(key_pick, (blocks, TOK_DEV, MAXNODES * N_LOCAL), 0, 1 << 20) * (MAXNODES * N_LOCAL)
    scores = scores + jnp.arange(MAXNODES * N_LOCAL, dtype=jnp.int32) + is_hot * (1 << 28)
    picked = lax.top_k(scores, TOP)[1]
    chosen_ids = jnp.take_along_axis(candidates, picked, axis=2)
    return chosen_ids.reshape(TOKENS, TOP).astype(jnp.int32)


def steps_of(stream_key, dims, cuts, smallest, top_value):
    def one(position, parts):
        steps = jax.random.uniform(jax.random.fold_in(jax.random.fold_in(stream_key, 6), position), (parts,), jnp.float32, smallest / len(cuts), top_value / len(cuts))
        return jnp.repeat(jnp.exp(steps), dims[position] // parts).reshape((-1,) + (1,) * (len(dims) - position - 1))

    loudness = one(*cuts[0])
    for cut in cuts[1:]:
        loudness = loudness * one(*cut)
    return loudness


def gaussian(key, shape, deviation, bound, pieces=(), kind=jnp.bfloat16):
    factor_of = steps_of(key, shape, pieces, -0.22, 0.18) if pieces else 1.0
    values = jax.random.normal(key, shape, jnp.float32) * deviation * factor_of
    return jnp.minimum(jnp.maximum(values, -bound), bound).astype(kind)


def setup_inputs(seed: int = 0, part: int = 0) -> dict:
    arg_keys = jax.random.split(jax.random.key(seed), 7)
    own_keys = jax.random.split(jax.random.fold_in(arg_keys[6], part), 7)
    return {
        "tokens": gaussian(own_keys[0], (TOKENS, D), 1.0, 6.0, ((0, 16),)),
        "gate_scores": jnp.clip(0.1 + 0.9 * jax.random.uniform(own_keys[1], (TOKENS, TOP), jnp.float32) ** steps_of(own_keys[1], (TOKENS, TOP), ((0, 16),), -0.2, 0.2), 0.1, 1.0),
        "expert_ids": draw_expert_ids(jax.random.fold_in(jax.random.fold_in(arg_keys[6], part), 71), part),
        "w_gate": gaussian(arg_keys[3], (EXPERTS, D, FF), D ** -0.5, 0.09375, ((0, 16),)),
        "w_up": gaussian(arg_keys[4], (EXPERTS, D, FF), D ** -0.5, 0.09375, ((0, 16),)),
        "w_down": gaussian(arg_keys[5], (EXPERTS, FF, D), FF ** -0.5, 0.1875, ((0, 16),)),
    }


def quantize(tokens):
    count_rows, width = tokens.shape
    tiles = tokens.astype(jnp.float32).reshape(count_rows, width // 128, 128)
    largest = jnp.max(jnp.abs(tiles), axis=-1)
    tile_scale = ((largest + 1e-6) / 448.0).astype(jnp.bfloat16)
    scale_wide = lax.optimization_barrier(tile_scale).astype(jnp.float32)
    quantized = (tiles / scale_wide[..., None]).astype(jnp.bfloat16)
    return quantized.reshape(count_rows, width), tile_scale


def restore(quantized, tile_scale):
    dims_all = quantized.shape
    tiles = quantized.reshape(dims_all[:-1] + (dims_all[-1] // 128, 128)).astype(jnp.float32)
    return (tiles * tile_scale.astype(jnp.float32)[..., None]).reshape(dims_all).astype(jnp.bfloat16)


def expert_rows(row_block, gate_matrix, up_matrix, down_matrix):
    gate_act = jnp.dot(row_block, gate_matrix, preferred_element_type=jnp.float32)
    up_act = jnp.dot(row_block, up_matrix, preferred_element_type=jnp.float32)
    hidden = (jax.nn.silu(gate_act) * up_act).astype(jnp.bfloat16)
    return jnp.dot(hidden, down_matrix, preferred_element_type=jnp.float32).astype(jnp.bfloat16)


def reference(tokens, gate_scores, expert_ids, w_gate, w_up, w_down):
    quantized, tile_scale = quantize(tokens)
    restored = restore(quantized, tile_scale)
    gates = (2.5 * gate_scores / jnp.sum(gate_scores, axis=-1, keepdims=True)).astype(jnp.bfloat16)
    gate_flat = lax.optimization_barrier(gates).astype(jnp.float32).reshape(-1)
    flat_ids = expert_ids.reshape(-1).astype(jnp.int32)
    sorted_pos = jnp.argsort(flat_ids, stable=True).astype(jnp.int32)
    expert_load = jnp.sum((flat_ids[None, :] == jnp.arange(EXPERTS, dtype=jnp.int32)[:, None]).astype(jnp.int32), axis=1).astype(jnp.int32)
    expert_start = (jnp.cumsum(expert_load) - expert_load).astype(jnp.int32)
    most_rows = EXPERTS * CAP
    padded_pos = jnp.concatenate([sorted_pos, jnp.zeros((most_rows,), jnp.int32)])

    def one_expert(total, expert):
        flat_pos = lax.dynamic_slice(padded_pos, (expert_start[expert],), (most_rows,)).astype(jnp.int32)
        is_live = jnp.arange(most_rows, dtype=jnp.int32) < expert_load[expert]
        token_pos = (flat_pos // TOP).astype(jnp.int32)
        result = expert_rows(restored[token_pos], w_gate[expert], w_up[expert], w_down[expert])
        weight = jnp.where(is_live, gate_flat[flat_pos], jnp.zeros_like(gate_flat[flat_pos]))
        return total.at[token_pos].add(result.astype(jnp.float32) * weight[:, None]), None

    mixed, unused = lax.scan(one_expert, jnp.zeros((TOKENS, D), jnp.float32), jnp.arange(EXPERTS, dtype=jnp.int32))
    return mixed.astype(jnp.bfloat16)
```

```python
import functools

import jax
import jax.numpy as jnp
from jax import lax
from jax.experimental import pallas as pl
from jax.experimental.pallas import tpu as pltpu
from jax.sharding import PartitionSpec as P

MAXNODES = 2
MESH = pl.DeviceIdType.MESH
LANES = 128


def kernel(
    nodes,
    tokens_ref, ids_ref, score_ref, wg_ref, wu_ref, wd_ref,
    out_ref,
    pick_ref, gate_ref, wg, wu, wd, sent, tok, gts, hid, part, rx, ry, dg0, dg1, ret,
    w_sem, ssem, rsem, gssem, grsem,
):
    group, cap, width = tok.shape[1:]
    half = (width // LANES // 2) * LANES
    node = lax.axis_index("node")
    local = lax.axis_index("local")
    low, high = pl.ds(0, half), pl.ds(half, width - half)
    x_dev, y_dev = {"local": local ^ 1}, {"local": local ^ 2}

    def remote(k, which, src, dst, dev):
        return pltpu.make_async_remote_copy(
            src_ref=src, dst_ref=dst, send_sem=ssem.at[which, k], recv_sem=rsem.at[which, k],
            device_id=dev, device_id_type=MESH,
        )

    def copies(k):
        z_dev = {"node": node ^ k}
        return [
            lambda: remote(k, 0, sent.at[k, :, low], tok.at[k, 0, :, low], z_dev),
            lambda: remote(k, 1, tok.at[k, 0, :, low], tok.at[k, 1, :, low], x_dev),
            lambda: remote(k, 2, tok.at[k, 0, :, high], tok.at[k, 1, :, high], x_dev),
            lambda: remote(k, 3, tok.at[k, 0, :, high], tok.at[k, 2, :, high], y_dev),
            lambda: remote(k, 4, tok.at[k, 0, :, low], tok.at[k, 2, :, low], y_dev),
            lambda: remote(k, 5, tok.at[k, 1, :, low], tok.at[k, 3, :, low], y_dev),
            lambda: remote(k, 6, tok.at[k, 2, :, high], tok.at[k, 3, :, high], x_dev),
            lambda: remote(k, 7, part.at[k, 3, :, low], dg0.at[k], y_dev),
            lambda: remote(k, 8, part.at[k, 3, :, high], dg1.at[k], x_dev),
            lambda: remote(k, 9, part.at[k, 1, :, high], rx.at[k, :, high], x_dev),
            lambda: remote(k, 10, part.at[k, 2, :, low], ry.at[k, :, low], y_dev),
            lambda: remote(k, 11, part.at[k, 1, :, low], rx.at[k, :, low], x_dev),
            lambda: remote(k, 12, part.at[k, 2, :, high], ry.at[k, :, high], y_dev),
            lambda: remote(k, 13, part.at[k, 0, :, low], ret.at[k, :, low], z_dev),
            lambda: remote(k, 14, sent.at[k, :, high], tok.at[k, 0, :, high], z_dev),
            lambda: remote(k, 15, part.at[k, 0, :, high], ret.at[k, :, high], z_dev),
        ]

    def start(k, *which):
        for i in which:
            copies(k)[i]().start()

    def arrived(k, *which):
        for i in which:
            copies(k)[i]().wait_recv()

    def gate_copy(k, r):
        return pltpu.make_async_remote_copy(
            src_ref=gate_ref.at[k], dst_ref=gts.at[k, r],
            send_sem=gssem.at[k, r], recv_sem=grsem.at[k, r],
            device_id={"node": node ^ k, "local": local ^ r}, device_id_type=MESH,
        )

    def spread(k):
        arrived(k, 0)
        start(k, 1, 4)
        arrived(k, 14)
        start(k, 3, 2)

    def forward(k):
        arrived(k, 1)
        start(k, 5)
        arrived(k, 3)
        start(k, 6)

    def up(k):
        rows = tok[k].reshape(group * cap, width)
        tile = 256

        @pl.loop(0, wg.shape[1] // tile)
        def _(j):
            cols = pl.ds(pl.multiple_of(j * tile, tile), tile)
            a = jnp.dot(rows, wg[:, cols], preferred_element_type=jnp.float32)
            b = jnp.dot(rows, wu[:, cols], preferred_element_type=jnp.float32)
            hid[:, cols] = (a / (1.0 + jnp.exp(-a)) * b).astype(jnp.bfloat16)

    def down(k):
        gates = gts[k].astype(jnp.float32)
        row = lax.broadcasted_iota(jnp.int32, gates.shape, 1)
        flat = jnp.sum(jnp.where(row == local, gates, 0.0), axis=1, keepdims=True)
        wide = jnp.broadcast_to(flat, (group, cap, LANES))
        slot = lax.broadcasted_iota(jnp.int32, wide.shape, 1)
        lane = lax.broadcasted_iota(jnp.int32, wide.shape, 2)
        mine = jnp.sum(jnp.where(slot == lane, wide, 0.0), axis=2, keepdims=True)
        tile = 512

        @pl.loop(0, width // tile)
        def _(j):
            cols = pl.ds(pl.multiple_of(j * tile, tile), tile)
            y = jnp.dot(hid[...], wd[:, cols], preferred_element_type=jnp.float32)
            part[k, :, :, cols] = (y.reshape(group, cap, tile) * mine).astype(jnp.bfloat16)

    def add(a, b):
        return (a.astype(jnp.float32) + b.astype(jnp.float32)).astype(jnp.bfloat16)

    def give(k):
        start(k, 7, 8, 10, 9)

    def relay(k):
        arrived(k, 7)
        part[k, 1, :, low] = add(part[k, 1, :, low], dg0[k])
        start(k, 11)
        arrived(k, 8)
        part[k, 2, :, high] = add(part[k, 2, :, high], dg1[k])
        start(k, 12)

    def settle(k, cols):
        arrived(k, *((10, 11) if cols is low else (9, 12)))
        return (
            part[k, 0, :, cols].astype(jnp.float32)
            + rx[k, :, cols].astype(jnp.float32)
            + ry[k, :, cols].astype(jnp.float32)
        ).astype(jnp.bfloat16)

    def finish(k):
        part[k, 0, :, low] = settle(k, low)
        start(k, 13)
        part[k, 0, :, high] = settle(k, high)
        start(k, 15)

    w_copies = [
        pltpu.make_async_copy(wg_ref.at[0], wg, w_sem.at[0]),
        pltpu.make_async_copy(wu_ref.at[0], wu, w_sem.at[1]),
        pltpu.make_async_copy(wd_ref.at[0], wd, w_sem.at[2]),
    ]
    others = [(k, r) for k in range(nodes) for r in range(group) if (k, r) != (0, 0)]
    barrier = pltpu.get_barrier_semaphore()
    for k, r in others:
        pl.semaphore_signal(
            barrier, inc=1, device_id={"node": node ^ k, "local": local ^ r}, device_id_type=MESH
        )

    step = 2 * LANES

    def restore(first, count):
        @pl.loop(first, first + count)
        def _(j):
            cols = pl.ds(pl.multiple_of(j * step, step), step)
            x = tokens_ref[:, cols].astype(jnp.float32)
            tiles = []
            for t in range(2):
                v = x[:, t * LANES:(t + 1) * LANES]
                largest = jnp.max(jnp.abs(v), axis=1, keepdims=True)
                scale = ((largest + 1e-06) / 448.0).astype(jnp.bfloat16).astype(jnp.float32)
                quantized = (v / scale).astype(jnp.bfloat16).astype(jnp.float32)
                tiles.append((quantized * scale).astype(jnp.bfloat16))
            chosen = jnp.dot(
                pick_ref[...], jnp.concatenate(tiles, axis=1), preferred_element_type=jnp.float32
            ).astype(jnp.bfloat16)
            tok[0, 0, :, cols] = chosen[:cap]
            sent[:, :, cols] = chosen.reshape(nodes, cap, step)

    rows = tokens_ref.shape[0]
    ids = ids_ref[...]
    score = score_ref[...]
    gates = (2.5 * score / jnp.sum(score, axis=0, keepdims=True)).astype(jnp.bfloat16)
    gates = gates.astype(jnp.float32)
    before = (
        lax.broadcasted_iota(jnp.int32, (rows, rows), 0)
        < lax.broadcasted_iota(jnp.int32, (rows, rows), 1)
    ).astype(jnp.float32).astype(jnp.bfloat16)
    for k in range(nodes):
        sums = [
            jnp.sum(jnp.where(ids == (node ^ k) * group + r, 1.0, 0.0), axis=0, keepdims=True)
            for r in range(group)
        ]
        weights = [
            jnp.sum(jnp.where(ids == (node ^ k) * group + r, gates, 0.0), axis=0, keepdims=True)
            for r in range(group)
        ]
        hit = jnp.minimum(functools.reduce(lambda a, b: a + b, sums), 1.0)
        rank = jnp.dot(
            jnp.broadcast_to(hit, (16, rows)).astype(jnp.bfloat16), before,
            preferred_element_type=jnp.float32,
        )[0:1].astype(jnp.int32)
        slot = lax.broadcasted_iota(jnp.int32, (LANES, rows), 0)
        chosen = jnp.where((slot == rank) & (slot < cap), hit, 0.0)
        line = lax.broadcasted_iota(jnp.int32, (16, rows), 0)
        table = jnp.zeros((16, rows), jnp.float32)
        for r in range(group):
            table = jnp.where(line == r, weights[r], table)
        chosen = chosen.astype(jnp.bfloat16)
        pick_ref[k * cap:(k + 1) * cap] = chosen[:cap]
        gate_ref[k] = lax.dot_general(
            table.astype(jnp.bfloat16), chosen, (((1,), (1,)), ((), ())),
            preferred_element_type=jnp.float32,
        ).astype(jnp.bfloat16)
    gts[0, 0] = gate_ref[0]
    restore(0, half // step)
    pl.semaphore_wait(barrier, nodes * group - 1)
    start(0, 1, 4)
    start(1, 0)
    for k, r in others:
        gate_copy(k, r).start()
    restore(half // step, (width - half) // step)
    start(1, 14)
    start(0, 3, 2)
    for k in range(2, nodes):
        start(k, 0)
        start(k, 14)
    for c in w_copies:
        c.start()
    forward(0)

    for k in range(nodes):
        if k + 1 < nodes:
            spread(k + 1)
        arrived(k, 2, 4, 5, 6)
        if k == 0:
            w_copies[0].wait()
            w_copies[1].wait()
        up(k)
        if k + 1 < nodes:
            forward(k + 1)
        if k == 0:
            w_copies[2].wait()
        for r in range(group):
            if (k, r) != (0, 0):
                gate_copy(k, r).wait_recv()
        down(k)
        if k >= 3:
            relay(k - 1)
        if k >= 2:
            give(k)
        if k >= 4:
            finish(k - 2)
    give(1)
    relay(nodes - 1)
    finish(nodes - 2)
    relay(1)
    give(0)
    finish(nodes - 1)
    finish(1)
    relay(0)
    ret[0, :, low] = settle(0, low)
    ret[0, :, high] = settle(0, high)

    @pl.loop(1, nodes)
    def _(k):
        arrived(k, 13, 15)

    tile = 512
    blocks = nodes * cap

    @pl.loop(0, width // tile)
    def _(j):
        cols = pl.ds(pl.multiple_of(j * tile, tile), tile)
        vals = ret[:, :, cols].reshape(blocks, tile)
        out_ref[:, cols] = lax.dot_general(
            pick_ref[...], vals, (((0,), (0,)), ((), ())), preferred_element_type=jnp.float32
        ).astype(jnp.bfloat16)

    for i in range(1, 13):
        @pl.loop(0, nodes)
        def _(k):
            copies(k)[i]().wait_send()

    for k, r in others:
        gate_copy(k, r).wait_send()

    for i in (0, 13, 14, 15):
        @pl.loop(1, nodes)
        def _(k):
            copies(k)[i]().wait_send()


def per_device(tokens, gate_scores, expert_ids, w_gate, w_up, w_down):
    rows, width = tokens.shape
    nodes = lax.axis_size("node")
    group = lax.axis_size("local")
    cap = MAXNODES * rows // nodes
    hidden = w_gate.shape[2]

    half = (width // LANES // 2) * LANES
    bf16 = jnp.bfloat16
    anywhere = pl.BlockSpec(memory_space=pl.ANY)
    vmem = pl.BlockSpec(memory_space=pltpu.VMEM)
    pairs = nodes * group * cap
    return pl.pallas_call(
        functools.partial(kernel, nodes),
        out_shape=pltpu.VMEM((rows, width), bf16),
        in_specs=[vmem] * 3 + [anywhere] * 3,
        out_specs=vmem,
        scratch_shapes=[
            pltpu.VMEM((nodes * cap, rows), bf16),
            pltpu.VMEM((nodes, 16, LANES), bf16),
            pltpu.VMEM((width, hidden), bf16),
            pltpu.VMEM((width, hidden), bf16),
            pltpu.VMEM((hidden, width), bf16),
            pltpu.VMEM((nodes, cap, width), bf16),
            pltpu.VMEM((nodes, group, cap, width), bf16),
            pltpu.VMEM((nodes, group, 16, LANES), bf16),
            pltpu.VMEM((group * cap, hidden), bf16),
            pltpu.VMEM((nodes, group, cap, width), bf16),
            pltpu.VMEM((nodes, cap, width), bf16),
            pltpu.VMEM((nodes, cap, width), bf16),
            pltpu.VMEM((nodes, cap, half), bf16),
            pltpu.VMEM((nodes, cap, width - half), bf16),
            pltpu.VMEM((nodes, cap, width), bf16),
            pltpu.SemaphoreType.DMA((3,)),
            pltpu.SemaphoreType.DMA((16, nodes)),
            pltpu.SemaphoreType.DMA((16, nodes)),
            pltpu.SemaphoreType.DMA((nodes, group)),
            pltpu.SemaphoreType.DMA((nodes, group)),
        ],
        compiler_params=pltpu.CompilerParams(
            collective_id=0, has_side_effects=True, vmem_limit_bytes=56*2**20
        ),
        cost_estimate=pl.CostEstimate(
            flops=6 * pairs * width * hidden,
            bytes_accessed=6 * width * hidden,
            transcendentals=pairs * hidden,
        ),
        name="routed_experts",
    )(tokens, expert_ids.T, gate_scores.T, w_gate, w_up, w_down)


def solution(mesh):
    in_specs = (
        P(("dp", "node", "local"), None),
        P(("dp", "node", "local"), None),
        P(("dp", "node", "local"), None),
        P(("node", "local"), None, None),
        P(("node", "local"), None, None),
        P(("node", "local"), None, None),
    )
    out_specs = P(("dp", "node", "local"), None)
    return jax.shard_map(
        per_device, mesh=mesh, in_specs=in_specs, out_specs=out_specs, check_vma=False
    )
```

```python
import functools

import jax
import jax.numpy as jnp
from jax import lax
from jax.experimental import pallas as pl
from jax.experimental.pallas import tpu as pltpu
from jax.sharding import PartitionSpec as P

MAXNODES = 2
MESH = pl.DeviceIdType.MESH
LANES = 128


def kernel(
    nodes,
    tokens_ref, ids_ref, score_ref, wg_ref, wu_ref, wd_ref,
    out_ref,
    pick_ref, gate_ref, wg, wu, wd, sent, tok, gts, hid, part, rx, ry, dg0, dg1, ret,
    w_sem, ssem, rsem, gssem, grsem,
):
    group, cap, width = tok.shape[1:]
    half = (width // LANES // 2) * LANES
    node = lax.axis_index("node")
    local = lax.axis_index("local")
    low, high = pl.ds(0, half), pl.ds(half, width - half)
    x_dev, y_dev = {"local": local ^ 1}, {"local": local ^ 2}

    def remote(k, which, src, dst, dev):
        return pltpu.make_async_remote_copy(
            src_ref=src, dst_ref=dst, send_sem=ssem.at[which, k], recv_sem=rsem.at[which, k],
            device_id=dev, device_id_type=MESH,
        )

    def copies(k):
        z_dev = {"node": node ^ k}
        return [
            lambda: remote(k, 0, sent.at[k, :, low], tok.at[k, 0, :, low], z_dev),
            lambda: remote(k, 1, tok.at[k, 0, :, low], tok.at[k, 1, :, low], x_dev),
            lambda: remote(k, 2, tok.at[k, 0, :, high], tok.at[k, 1, :, high], x_dev),
            lambda: remote(k, 3, tok.at[k, 0, :, high], tok.at[k, 2, :, high], y_dev),
            lambda: remote(k, 4, tok.at[k, 0, :, low], tok.at[k, 2, :, low], y_dev),
            lambda: remote(k, 5, tok.at[k, 1, :, low], tok.at[k, 3, :, low], y_dev),
            lambda: remote(k, 6, tok.at[k, 2, :, high], tok.at[k, 3, :, high], x_dev),
            lambda: remote(k, 7, part.at[k, 3, :, low], dg0.at[k], y_dev),
            lambda: remote(k, 8, part.at[k, 3, :, high], dg1.at[k], x_dev),
            lambda: remote(k, 9, part.at[k, 1, :, high], rx.at[k, :, high], x_dev),
            lambda: remote(k, 10, part.at[k, 2, :, low], ry.at[k, :, low], y_dev),
            lambda: remote(k, 11, part.at[k, 1, :, low], rx.at[k, :, low], x_dev),
            lambda: remote(k, 12, part.at[k, 2, :, high], ry.at[k, :, high], y_dev),
            lambda: remote(k, 13, part.at[k, 0, :, low], ret.at[k, :, low], z_dev),
            lambda: remote(k, 14, sent.at[k, :, high], tok.at[k, 0, :, high], z_dev),
            lambda: remote(k, 15, part.at[k, 0, :, high], ret.at[k, :, high], z_dev),
        ]

    def start(k, *which):
        for i in which:
            copies(k)[i]().start()

    def arrived(k, *which):
        for i in which:
            copies(k)[i]().wait_recv()

    def gate_copy(k, r):
        return pltpu.make_async_remote_copy(
            src_ref=gate_ref.at[k], dst_ref=gts.at[k, r],
            send_sem=gssem.at[k, r], recv_sem=grsem.at[k, r],
            device_id={"node": node ^ k, "local": local ^ r}, device_id_type=MESH,
        )

    def spread(k):
        arrived(k, 0)
        start(k, 1, 4)
        arrived(k, 14)
        start(k, 3, 2)

    def forward(k):
        arrived(k, 1)
        start(k, 5)
        arrived(k, 3)
        start(k, 6)

    def up(k):
        rows = tok[k].reshape(group * cap, width)
        tile = 256

        @pl.loop(0, wg.shape[1] // tile)
        def _(j):
            cols = pl.ds(pl.multiple_of(j * tile, tile), tile)
            a = jnp.dot(rows, wg[:, cols], preferred_element_type=jnp.float32)
            b = jnp.dot(rows, wu[:, cols], preferred_element_type=jnp.float32)
            hid[:, cols] = (a / (1.0 + jnp.exp(-a)) * b).astype(jnp.bfloat16)

    def down(k):
        gates = gts[k].astype(jnp.float32)
        row = lax.broadcasted_iota(jnp.int32, gates.shape, 1)
        flat = jnp.sum(jnp.where(row == local, gates, 0.0), axis=1, keepdims=True)
        wide = jnp.broadcast_to(flat, (group, cap, LANES))
        slot = lax.broadcasted_iota(jnp.int32, wide.shape, 1)
        lane = lax.broadcasted_iota(jnp.int32, wide.shape, 2)
        mine = jnp.sum(jnp.where(slot == lane, wide, 0.0), axis=2, keepdims=True)
        tile = 512

        @pl.loop(0, width // tile)
        def _(j):
            cols = pl.ds(pl.multiple_of(j * tile, tile), tile)
            y = jnp.dot(hid[...], wd[:, cols], preferred_element_type=jnp.float32)
            part[k, :, :, cols] = (y.reshape(group, cap, tile) * mine).astype(jnp.bfloat16)

    def add(a, b):
        return (a.astype(jnp.float32) + b.astype(jnp.float32)).astype(jnp.bfloat16)

    def give(k):
        start(k, 7, 8, 10, 9)

    def relay(k):
        arrived(k, 7)
        part[k, 1, :, low] = add(part[k, 1, :, low], dg0[k])
        start(k, 11)
        arrived(k, 8)
        part[k, 2, :, high] = add(part[k, 2, :, high], dg1[k])
        start(k, 12)

    def settle(k, cols):
        arrived(k, *((10, 11) if cols is low else (9, 12)))
        return (
            part[k, 0, :, cols].astype(jnp.float32)
            + rx[k, :, cols].astype(jnp.float32)
            + ry[k, :, cols].astype(jnp.float32)
        ).astype(jnp.bfloat16)

    def finish(k):
        part[k, 0, :, low] = settle(k, low)
        start(k, 13)
        part[k, 0, :, high] = settle(k, high)
        start(k, 15)

    w_copies = [
        pltpu.make_async_copy(wg_ref.at[0], wg, w_sem.at[0]),
        pltpu.make_async_copy(wu_ref.at[0], wu, w_sem.at[1]),
        pltpu.make_async_copy(wd_ref.at[0], wd, w_sem.at[2]),
    ]
    others = [(k, r) for k in range(nodes) for r in range(group) if (k, r) != (0, 0)]
    barrier = pltpu.get_barrier_semaphore()
    for k, r in others:
        pl.semaphore_signal(
            barrier, inc=1, device_id={"node": node ^ k, "local": local ^ r}, device_id_type=MESH
        )

    step = 2 * LANES

    def restore(first, count):
        @pl.loop(first, first + count)
        def _(j):
            cols = pl.ds(pl.multiple_of(j * step, step), step)
            x = tokens_ref[:, cols].astype(jnp.float32)
            tiles = []
            for t in range(2):
                v = x[:, t * LANES:(t + 1) * LANES]
                largest = jnp.max(jnp.abs(v), axis=1, keepdims=True)
                scale = ((largest + 1e-06) / 448.0).astype(jnp.bfloat16).astype(jnp.float32)
                quantized = (v / scale).astype(jnp.bfloat16).astype(jnp.float32)
                tiles.append((quantized * scale).astype(jnp.bfloat16))
            chosen = jnp.dot(
                pick_ref[...], jnp.concatenate(tiles, axis=1), preferred_element_type=jnp.float32
            ).astype(jnp.bfloat16)
            tok[0, 0, :, cols] = chosen[:cap]
            sent[:, :, cols] = chosen.reshape(nodes, cap, step)

    rows = tokens_ref.shape[0]
    ids = ids_ref[...]
    score = score_ref[...]
    gates = (2.5 * score / jnp.sum(score, axis=0, keepdims=True)).astype(jnp.bfloat16)
    gates = gates.astype(jnp.float32)
    before = (
        lax.broadcasted_iota(jnp.int32, (rows, rows), 0)
        < lax.broadcasted_iota(jnp.int32, (rows, rows), 1)
    ).astype(jnp.float32).astype(jnp.bfloat16)
    for k in range(nodes):
        sums = [
            jnp.sum(jnp.where(ids == (node ^ k) * group + r, 1.0, 0.0), axis=0, keepdims=True)
            for r in range(group)
        ]
        weights = [
            jnp.sum(jnp.where(ids == (node ^ k) * group + r, gates, 0.0), axis=0, keepdims=True)
            for r in range(group)
        ]
        hit = jnp.minimum(functools.reduce(lambda a, b: a + b, sums), 1.0)
        rank = jnp.dot(
            jnp.broadcast_to(hit, (16, rows)).astype(jnp.bfloat16), before,
            preferred_element_type=jnp.float32,
        )[0:1].astype(jnp.int32)
        slot = lax.broadcasted_iota(jnp.int32, (LANES, rows), 0)
        chosen = jnp.where((slot == rank) & (slot < cap), hit, 0.0)
        line = lax.broadcasted_iota(jnp.int32, (16, rows), 0)
        table = jnp.zeros((16, rows), jnp.float32)
        for r in range(group):
            table = jnp.where(line == r, weights[r], table)
        chosen = chosen.astype(jnp.bfloat16)
        pick_ref[k * cap:(k + 1) * cap] = chosen[:cap]
        gate_ref[k] = lax.dot_general(
            table.astype(jnp.bfloat16), chosen, (((1,), (1,)), ((), ())),
            preferred_element_type=jnp.float32,
        ).astype(jnp.bfloat16)
    gts[0, 0] = gate_ref[0]
    restore(0, half // step)
    pl.semaphore_wait(barrier, nodes * group - 1)
    start(0, 1, 4)
    start(1, 0)
    for k, r in others:
        gate_copy(k, r).start()
    restore(half // step, (width - half) // step)
    start(1, 14)
    start(0, 3, 2)
    for k in range(2, nodes):
        start(k, 0)
        start(k, 14)
    for c in w_copies:
        c.start()
    forward(0)

    for k in range(nodes):
        if k + 1 < nodes:
            spread(k + 1)
        arrived(k, 2, 4, 5, 6)
        if k == 0:
            w_copies[0].wait()
            w_copies[1].wait()
        up(k)
        if k + 1 < nodes:
            forward(k + 1)
        if k == 0:
            w_copies[2].wait()
        for r in range(group):
            if (k, r) != (0, 0):
                gate_copy(k, r).wait_recv()
        down(k)
        if k >= 3:
            relay(k - 1)
        if k >= 2:
            give(k)
        if k >= 4:
            finish(k - 2)
    finish(nodes - 2)
    relay(nodes - 1)
    give(1)
    finish(nodes - 1)
    relay(1)
    give(0)
    finish(1)
    relay(0)

    @pl.loop(1, nodes)
    def _(k):
        arrived(k, 13, 15)

    tile = 512
    flipped = pick_ref[...].astype(jnp.float32).T.astype(jnp.bfloat16)
    own_pick, far_pick = flipped[:, :cap], flipped[:, cap:]

    @pl.loop(0, width // tile)
    def _(j):
        cols = pl.ds(pl.multiple_of(j * tile, tile), tile)
        vals = ret[1:, :, cols].reshape((nodes - 1) * cap, tile)
        out_ref[:, cols] = jnp.dot(
            far_pick, vals, preferred_element_type=jnp.float32
        ).astype(jnp.bfloat16)

    for cols in (low, high):
        own = jnp.dot(own_pick, settle(0, cols), preferred_element_type=jnp.float32)
        out_ref[:, cols] = (out_ref[:, cols].astype(jnp.float32) + own).astype(jnp.bfloat16)

    for i in range(1, 13):
        @pl.loop(0, nodes)
        def _(k):
            copies(k)[i]().wait_send()

    for k, r in others:
        gate_copy(k, r).wait_send()

    for i in (0, 13, 14, 15):
        @pl.loop(1, nodes)
        def _(k):
            copies(k)[i]().wait_send()


def per_device(tokens, gate_scores, expert_ids, w_gate, w_up, w_down):
    rows, width = tokens.shape
    nodes = lax.axis_size("node")
    group = lax.axis_size("local")
    cap = MAXNODES * rows // nodes
    hidden = w_gate.shape[2]

    half = (width // LANES // 2) * LANES
    bf16 = jnp.bfloat16
    anywhere = pl.BlockSpec(memory_space=pl.ANY)
    vmem = pl.BlockSpec(memory_space=pltpu.VMEM)
    pairs = nodes * group * cap
    return pl.pallas_call(
        functools.partial(kernel, nodes),
        out_shape=pltpu.VMEM((rows, width), bf16),
        in_specs=[vmem] * 3 + [anywhere] * 3,
        out_specs=vmem,
        scratch_shapes=[
            pltpu.VMEM((nodes * cap, rows), bf16),
            pltpu.VMEM((nodes, 16, LANES), bf16),
            pltpu.VMEM((width, hidden), bf16),
            pltpu.VMEM((width, hidden), bf16),
            pltpu.VMEM((hidden, width), bf16),
            pltpu.VMEM((nodes, cap, width), bf16),
            pltpu.VMEM((nodes, group, cap, width), bf16),
            pltpu.VMEM((nodes, group, 16, LANES), bf16),
            pltpu.VMEM((group * cap, hidden), bf16),
            pltpu.VMEM((nodes, group, cap, width), bf16),
            pltpu.VMEM((nodes, cap, width), bf16),
            pltpu.VMEM((nodes, cap, width), bf16),
            pltpu.VMEM((nodes, cap, half), bf16),
            pltpu.VMEM((nodes, cap, width - half), bf16),
            pltpu.VMEM((nodes, cap, width), bf16),
            pltpu.SemaphoreType.DMA((3,)),
            pltpu.SemaphoreType.DMA((16, nodes)),
            pltpu.SemaphoreType.DMA((16, nodes)),
            pltpu.SemaphoreType.DMA((nodes, group)),
            pltpu.SemaphoreType.DMA((nodes, group)),
        ],
        compiler_params=pltpu.CompilerParams(
            collective_id=0, has_side_effects=True, vmem_limit_bytes=56*2**20
        ),
        cost_estimate=pl.CostEstimate(
            flops=6 * pairs * width * hidden,
            bytes_accessed=6 * width * hidden,
            transcendentals=pairs * hidden,
        ),
        name="routed_experts",
    )(tokens, expert_ids.T, gate_scores.T, w_gate, w_up, w_down)


def solution(mesh):
    in_specs = (
        P(("dp", "node", "local"), None),
        P(("dp", "node", "local"), None),
        P(("dp", "node", "local"), None),
        P(("node", "local"), None, None),
        P(("node", "local"), None, None),
        P(("node", "local"), None, None),
    )
    out_specs = P(("dp", "node", "local"), None)
    return jax.shard_map(
        per_device, mesh=mesh, in_specs=in_specs, out_specs=out_specs, check_vma=False
    )
```

```python
import functools

import jax
import jax.numpy as jnp
from jax import lax
from jax.experimental import pallas as pl
from jax.experimental.pallas import tpu as pltpu
from jax.sharding import PartitionSpec as P

MAXNODES = 2
MESH = pl.DeviceIdType.MESH
LANES = 128


def kernel(
    nodes,
    tokens_ref, ids_ref, score_ref, wg_ref, wu_ref, wd_ref,
    out_ref,
    pick_ref, gate_ref, wg, wu, wd, sent, tok, gts, hid, part, rx, ry, dg0, dg1, ret,
    w_sem, ssem, rsem, gssem, grsem,
):
    group, cap, width = tok.shape[1:]
    half = (width // LANES // 2) * LANES
    node = lax.axis_index("node")
    local = lax.axis_index("local")
    core = lax.axis_index("dp")
    low, high = pl.ds(0, half), pl.ds(half, width - half)
    x_dev, y_dev = {"local": local ^ 1}, {"local": local ^ 2}

    def remote(k, which, src, dst, dev):
        return pltpu.make_async_remote_copy(
            src_ref=src, dst_ref=dst, send_sem=ssem.at[which, k], recv_sem=rsem.at[which, k],
            device_id=dev, device_id_type=MESH,
        )

    def copies(k):
        z_dev = {"node": node ^ k}
        return [
            lambda: remote(k, 0, sent.at[k, :, low], tok.at[k, 0, :, low], z_dev),
            lambda: remote(k, 1, tok.at[k, 0, :, low], tok.at[k, 1, :, low], x_dev),
            lambda: remote(k, 2, tok.at[k, 0, :, high], tok.at[k, 1, :, high], x_dev),
            lambda: remote(k, 3, tok.at[k, 0, :, high], tok.at[k, 2, :, high], y_dev),
            lambda: remote(k, 4, tok.at[k, 0, :, low], tok.at[k, 2, :, low], y_dev),
            lambda: remote(k, 5, tok.at[k, 1, :, low], tok.at[k, 3, :, low], y_dev),
            lambda: remote(k, 6, tok.at[k, 2, :, high], tok.at[k, 3, :, high], x_dev),
            lambda: remote(k, 7, part.at[k, 3, :, low], dg0.at[k], y_dev),
            lambda: remote(k, 8, part.at[k, 3, :, high], dg1.at[k], x_dev),
            lambda: remote(k, 9, part.at[k, 1, :, high], rx.at[k, :, high], x_dev),
            lambda: remote(k, 10, part.at[k, 2, :, low], ry.at[k, :, low], y_dev),
            lambda: remote(k, 11, part.at[k, 1, :, low], rx.at[k, :, low], x_dev),
            lambda: remote(k, 12, part.at[k, 2, :, high], ry.at[k, :, high], y_dev),
            lambda: remote(k, 13, part.at[k, 0, :, low], ret.at[k, :, low], z_dev),
            lambda: remote(k, 14, sent.at[k, :, high], tok.at[k, 0, :, high], z_dev),
            lambda: remote(k, 15, part.at[k, 0, :, high], ret.at[k, :, high], z_dev),
        ]

    def start(k, *which):
        for i in which:
            copies(k)[i]().start()

    def arrived(k, *which):
        for i in which:
            copies(k)[i]().wait_recv()

    def gate_copy(k, r):
        return pltpu.make_async_remote_copy(
            src_ref=gate_ref.at[k], dst_ref=gts.at[k, r],
            send_sem=gssem.at[k, r], recv_sem=grsem.at[k, r],
            device_id={"node": node ^ k, "local": local ^ r}, device_id_type=MESH,
        )

    def spread(k):
        arrived(k, 0)
        start(k, 1, 4)
        arrived(k, 14)
        start(k, 3, 2)

    def forward(k):
        arrived(k, 1)
        start(k, 5)
        arrived(k, 3)
        start(k, 6)

    def up(k):
        rows = tok[k].reshape(group * cap, width)
        tile = 256

        @pl.loop(0, wg.shape[1] // tile)
        def _(j):
            cols = pl.ds(pl.multiple_of(j * tile, tile), tile)
            a = jnp.dot(rows, wg[:, cols], preferred_element_type=jnp.float32)
            b = jnp.dot(rows, wu[:, cols], preferred_element_type=jnp.float32)
            hid[:, cols] = (a / (1.0 + jnp.exp(-a)) * b).astype(jnp.bfloat16)

    def down(k):
        gates = gts[k].astype(jnp.float32)
        row = lax.broadcasted_iota(jnp.int32, gates.shape, 1)
        flat = jnp.sum(jnp.where(row == local, gates, 0.0), axis=1, keepdims=True)
        wide = jnp.broadcast_to(flat, (group, cap, LANES))
        slot = lax.broadcasted_iota(jnp.int32, wide.shape, 1)
        lane = lax.broadcasted_iota(jnp.int32, wide.shape, 2)
        mine = jnp.sum(jnp.where(slot == lane, wide, 0.0), axis=2, keepdims=True)
        tile = 512

        @pl.loop(0, width // tile)
        def _(j):
            cols = pl.ds(pl.multiple_of(j * tile, tile), tile)
            y = jnp.dot(hid[...], wd[:, cols], preferred_element_type=jnp.float32)
            part[k, :, :, cols] = (y.reshape(group, cap, tile) * mine).astype(jnp.bfloat16)

    def add(a, b):
        return (a.astype(jnp.float32) + b.astype(jnp.float32)).astype(jnp.bfloat16)

    def give(k):
        start(k, 7, 8, 10, 9)

    def relay(k):
        arrived(k, 7)
        part[k, 1, :, low] = add(part[k, 1, :, low], dg0[k])
        start(k, 11)
        arrived(k, 8)
        part[k, 2, :, high] = add(part[k, 2, :, high], dg1[k])
        start(k, 12)

    def settle(k, cols):
        arrived(k, *((10, 11) if cols is low else (9, 12)))
        return (
            part[k, 0, :, cols].astype(jnp.float32)
            + rx[k, :, cols].astype(jnp.float32)
            + ry[k, :, cols].astype(jnp.float32)
        ).astype(jnp.bfloat16)

    def finish(k):
        part[k, 0, :, low] = settle(k, low)
        start(k, 13)
        part[k, 0, :, high] = settle(k, high)
        start(k, 15)

    w_copies = [
        pltpu.make_async_copy(wg_ref.at[0], wg, w_sem.at[0]),
        pltpu.make_async_copy(wu_ref.at[0], wu, w_sem.at[1]),
        pltpu.make_async_copy(wd_ref.at[0], wd, w_sem.at[2]),
    ]
    others = [(k, r) for k in range(nodes) for r in range(group) if (k, r) != (0, 0)]
    barrier = pltpu.get_barrier_semaphore()
    for k, r in others:
        pl.semaphore_signal(
            barrier, inc=1, device_id={"node": node ^ k, "local": local ^ r}, device_id_type=MESH
        )

    step = 2 * LANES

    def restore(first, count):
        @pl.loop(first, first + count)
        def _(j):
            cols = pl.ds(pl.multiple_of(j * step, step), step)
            x = tokens_ref[:, cols].astype(jnp.float32)
            tiles = []
            for t in range(2):
                v = x[:, t * LANES:(t + 1) * LANES]
                largest = jnp.max(jnp.abs(v), axis=1, keepdims=True)
                scale = ((largest + 1e-06) / 448.0).astype(jnp.bfloat16).astype(jnp.float32)
                quantized = (v / scale).astype(jnp.bfloat16).astype(jnp.float32)
                tiles.append((quantized * scale).astype(jnp.bfloat16))
            chosen = jnp.dot(
                pick_ref[...], jnp.concatenate(tiles, axis=1), preferred_element_type=jnp.float32
            ).astype(jnp.bfloat16)
            tok[0, 0, :, cols] = chosen[:cap]
            sent[:, :, cols] = chosen.reshape(nodes, cap, step)

    rows = tokens_ref.shape[0]
    ids = ids_ref[...]
    score = score_ref[...]
    gates = (2.5 * score / jnp.sum(score, axis=0, keepdims=True)).astype(jnp.bfloat16)
    gates = gates.astype(jnp.float32)
    before = (
        lax.broadcasted_iota(jnp.int32, (rows, rows), 0)
        < lax.broadcasted_iota(jnp.int32, (rows, rows), 1)
    ).astype(jnp.float32).astype(jnp.bfloat16)
    for k in range(nodes):
        sums = [
            jnp.sum(jnp.where(ids == (node ^ k) * group + r, 1.0, 0.0), axis=0, keepdims=True)
            for r in range(group)
        ]
        weights = [
            jnp.sum(jnp.where(ids == (node ^ k) * group + r, gates, 0.0), axis=0, keepdims=True)
            for r in range(group)
        ]
        hit = jnp.minimum(functools.reduce(lambda a, b: a + b, sums), 1.0)
        rank = jnp.dot(
            jnp.broadcast_to(hit, (16, rows)).astype(jnp.bfloat16), before,
            preferred_element_type=jnp.float32,
        )[0:1].astype(jnp.int32)
        slot = lax.broadcasted_iota(jnp.int32, (LANES, rows), 0)
        chosen = jnp.where((slot == rank) & (slot < cap), hit, 0.0)
        line = lax.broadcasted_iota(jnp.int32, (16, rows), 0)
        table = jnp.zeros((16, rows), jnp.float32)
        for r in range(group):
            table = jnp.where(line == r, weights[r], table)
        chosen = chosen.astype(jnp.bfloat16)
        pick_ref[k * cap:(k + 1) * cap] = chosen[:cap]
        gate_ref[k] = lax.dot_general(
            table.astype(jnp.bfloat16), chosen, (((1,), (1,)), ((), ())),
            preferred_element_type=jnp.float32,
        ).astype(jnp.bfloat16)
    gts[0, 0] = gate_ref[0]
    restore(0, half // step)
    pl.semaphore_wait(barrier, nodes * group - 1)
    start(0, 1, 4)
    start(1, 0)
    for k, r in others:
        gate_copy(k, r).start()
    restore(half // step, (width - half) // step)
    start(1, 14)
    start(0, 3, 2)
    for k in range(2, nodes):
        start(k, 0)
        start(k, 14)
    for c in w_copies:
        c.start()
    forward(0)

    for k in range(nodes):
        if k + 1 < nodes:
            spread(k + 1)
        arrived(k, 2, 4, 5, 6)
        if k == 0:
            w_copies[0].wait()
            w_copies[1].wait()
        up(k)
        if k + 1 == nodes - 1:
            @pl.when(core == 0)
            def _():
                start(1, 7, 8)

        if k + 1 < nodes:
            forward(k + 1)
        if k == 0:
            w_copies[2].wait()
        for r in range(group):
            if (k, r) != (0, 0):
                gate_copy(k, r).wait_recv()
        down(k)
        if k >= 3:
            relay(k - 1)
        if k >= 2:
            give(k)
        if k >= 4:
            finish(k - 2)
    finish(nodes - 2)
    relay(nodes - 1)
    start(1, 10, 9)

    @pl.when(core == 1)
    def _():
        start(1, 7, 8)

    finish(nodes - 1)
    relay(1)
    give(0)
    finish(1)
    relay(0)

    @pl.loop(1, nodes)
    def _(k):
        arrived(k, 13, 15)

    tile = 512
    flipped = pick_ref[...].astype(jnp.float32).T.astype(jnp.bfloat16)
    own_pick, far_pick = flipped[:, :cap], flipped[:, cap:]

    @pl.loop(0, width // tile)
    def _(j):
        cols = pl.ds(pl.multiple_of(j * tile, tile), tile)
        vals = ret[1:, :, cols].reshape((nodes - 1) * cap, tile)
        out_ref[:, cols] = jnp.dot(
            far_pick, vals, preferred_element_type=jnp.float32
        ).astype(jnp.bfloat16)

    for cols in (low, high):
        own = jnp.dot(own_pick, settle(0, cols), preferred_element_type=jnp.float32)
        out_ref[:, cols] = (out_ref[:, cols].astype(jnp.float32) + own).astype(jnp.bfloat16)

    for i in range(1, 13):
        @pl.loop(0, nodes)
        def _(k):
            copies(k)[i]().wait_send()

    for k, r in others:
        gate_copy(k, r).wait_send()

    for i in (0, 13, 14, 15):
        @pl.loop(1, nodes)
        def _(k):
            copies(k)[i]().wait_send()


def per_device(tokens, gate_scores, expert_ids, w_gate, w_up, w_down):
    rows, width = tokens.shape
    nodes = lax.axis_size("node")
    group = lax.axis_size("local")
    cap = MAXNODES * rows // nodes
    hidden = w_gate.shape[2]

    half = (width // LANES // 2) * LANES
    bf16 = jnp.bfloat16
    anywhere = pl.BlockSpec(memory_space=pl.ANY)
    vmem = pl.BlockSpec(memory_space=pltpu.VMEM)
    pairs = nodes * group * cap
    return pl.pallas_call(
        functools.partial(kernel, nodes),
        out_shape=pltpu.VMEM((rows, width), bf16),
        in_specs=[vmem] * 3 + [anywhere] * 3,
        out_specs=vmem,
        scratch_shapes=[
            pltpu.VMEM((nodes * cap, rows), bf16),
            pltpu.VMEM((nodes, 16, LANES), bf16),
            pltpu.VMEM((width, hidden), bf16),
            pltpu.VMEM((width, hidden), bf16),
            pltpu.VMEM((hidden, width), bf16),
            pltpu.VMEM((nodes, cap, width), bf16),
            pltpu.VMEM((nodes, group, cap, width), bf16),
            pltpu.VMEM((nodes, group, 16, LANES), bf16),
            pltpu.VMEM((group * cap, hidden), bf16),
            pltpu.VMEM((nodes, group, cap, width), bf16),
            pltpu.VMEM((nodes, cap, width), bf16),
            pltpu.VMEM((nodes, cap, width), bf16),
            pltpu.VMEM((nodes, cap, half), bf16),
            pltpu.VMEM((nodes, cap, width - half), bf16),
            pltpu.VMEM((nodes, cap, width), bf16),
            pltpu.SemaphoreType.DMA((3,)),
            pltpu.SemaphoreType.DMA((16, nodes)),
            pltpu.SemaphoreType.DMA((16, nodes)),
            pltpu.SemaphoreType.DMA((nodes, group)),
            pltpu.SemaphoreType.DMA((nodes, group)),
        ],
        compiler_params=pltpu.CompilerParams(
            collective_id=0, has_side_effects=True, vmem_limit_bytes=56*2**20
        ),
        cost_estimate=pl.CostEstimate(
            flops=6 * pairs * width * hidden,
            bytes_accessed=6 * width * hidden,
            transcendentals=pairs * hidden,
        ),
        name="routed_experts",
    )(tokens, expert_ids.T, gate_scores.T, w_gate, w_up, w_down)


def solution(mesh):
    in_specs = (
        P(("dp", "node", "local"), None),
        P(("dp", "node", "local"), None),
        P(("dp", "node", "local"), None),
        P(("node", "local"), None, None),
        P(("node", "local"), None, None),
        P(("node", "local"), None, None),
    )
    out_specs = P(("dp", "node", "local"), None)
    return jax.shard_map(
        per_device, mesh=mesh, in_specs=in_specs, out_specs=out_specs, check_vma=False
    )
```
